768 devices in a mesh: dp: 16 (over x, z_hi, core), fsdp: 48 (over z_lo, y).
Axes of the slice: x: 4, y: 8, z: 12 (z_hi: 2, z_lo: 6; z = z_hi * 6 + z_lo), core: 2. Of those that a mesh axis runs over, the one named last changes fastest.
Arguments:
- activations: bfloat16 [98304, 8192], P(('dp', 'fsdp')), may hold values from -6 to 6
- queries: bfloat16 [98304, 4096], P(('dp', 'fsdp')), may hold values from -5 to 5
- key_states: bfloat16 [98304, 512], P(('dp', 'fsdp')), may hold values from -5 to 5
- out_grads: bfloat16 [98304, 4096], P(('dp', 'fsdp')), may hold values from -6 to 6
- projector: bfloat16 [8192, 512], P('dp'), may hold values from -0.0625 to 0.0625
- lengths: int32 [16, 96], P('dp'), may hold values from 1 to 128, 6144 in all within a row
Outputs:
- value_grads: bfloat16 [98304, 512], P(('dp', 'fsdp'))
- gradient: float32 [512, 512], P('dp')
The draws below stay inside these ranges and needn't reach their ends.
All inputs are finite; a program needn't handle non-finite values.
Results may differ from the reference program's by a relative error of at most 0.0048.
Values may be sent and summed in bfloat16 or wider, within the bound.
A program may use at most 64 MiB of HBM per device.

```python
import math
import jax
import jax.numpy as jnp
import numpy as np
from jax import lax

D = 8192
HEADS = 32
KV = 4
HD = 128
RANK = 512
TOK_DEV = 128
SEQ = 6144
TOKENS = 98304
DOCS = 96
N_DP = 16
N_FSDP = 48


def base_values(key, columns):
    return jax.random.truncated_normal(key, -4.0, 4.0, (TOKENS, columns), jnp.float32)


def draw_queries(key, part):
    values = base_values(jax.random.fold_in(key, 21), HEADS * HD)
    return values.astype(jnp.bfloat16)


def draw_key_states(key, part):
    values = base_values(jax.random.fold_in(key, 33), KV * HD)
    return values.astype(jnp.bfloat16)


def block_scale(stream_key, shape, pieces, least, high):
    def one(position, blocks):
        heights = jax.random.uniform(jax.random.fold_in(jax.random.fold_in(stream_key, 6), position), (blocks,), jnp.float32, least / len(pieces), high / len(pieces))
        return jnp.repeat(jnp.exp(heights), shape[position] // blocks).reshape((-1,) + (1,) * (len(shape) - position - 1))

    loudness = one(*pieces[0])
    for cut in pieces[1:]:
        loudness = loudness * one(*cut)
    return loudness


def length_profile(count, total, bound, skew):
    loads = [(1 << 20) // math.isqrt(standing ** skew) + 1 for standing in range(2, count + 1)]
    spare, holding = total - bound - (count - 1), [1] * (count - 1)
    while spare > 0:
        free = [i for i in range(count - 1) if holding[i] < bound]
        pool, left = sum([loads[i] for i in free]), spare
        for i in free:
            extra = min(bound - holding[i], max(1, left * loads[i] // pool), spare)
            holding[i] = holding[i] + extra
            spare = spare - extra
    return np.array([bound] + holding)


def ragged(rng, number_of, total, reach, slope):
    if number_of == 2:
        one = jax.random.randint(rng, (), max(1, total - reach), min(reach, total - 1) + 1)
        return jnp.stack([one, total - one])
    sizes = jnp.asarray(length_profile(number_of, total, reach, slope), jnp.int32)
    couples = (number_of - 1) // 2
    donor, taker = sizes[1:1 + 2 * couples:2], sizes[2:2 + 2 * couples:2]
    margin = jnp.minimum(donor - 1, reach - taker)
    moved = jax.random.randint(jax.random.fold_in(rng, 1), (couples,), 0, 1 << 20) % (margin + 1)
    sizes = sizes.at[1:1 + 2 * couples:2].set(donor - moved).at[2:2 + 2 * couples:2].set(taker + moved)
    return sizes[jax.random.permutation(jax.random.fold_in(rng, 2), number_of)]


def bell_draw(key, dims, deviation, bound, split=(), kind=jnp.bfloat16):
    drawn = deviation * jax.random.normal(key, dims, jnp.float32)
    if split:
        drawn = drawn * block_scale(key, dims, split, -0.22, 0.18)
    return jnp.clip(drawn, -bound, bound).astype(kind)


def setup_inputs(seed: int = 0) -> dict:
    key_list = jax.random.split(jax.random.key(seed), 7)
    activations = bell_draw(key_list[0], (TOKENS, D), 1.0, 6.0, ((0, 768),))
    queries = draw_queries(jax.random.fold_in(key_list[6], 71), 0)
    key_states = draw_key_states(jax.random.fold_in(key_list[6], 71), 0)
    out_grads = bell_draw(key_list[3], (TOKENS, HEADS * HD), 1.0, 6.0, ((0, 768),))
    projector = bell_draw(key_list[4], (D, RANK), D ** -0.5, 0.0625, ((0, 16),))
    lengths = jax.vmap(lambda own: ragged(own, DOCS, SEQ, TOK_DEV, 2))(jax.random.split(key_list[5], N_DP)).reshape((N_DP, DOCS)).astype(jnp.int32)
    return {"activations": activations, "queries": queries, "key_states": key_states, "out_grads": out_grads, "projector": projector, "lengths": lengths}


def doc_index(positions, doc_ends):
    return lax.optimization_barrier(jnp.sum((doc_ends[None, :] <= positions[:, None]).astype(jnp.int32), axis=1))

def attend(queries_block, keys_both, grads_block, visible):
    row_count = queries_block.shape[0]
    query_heads = queries_block.reshape(row_count, KV, HEADS // KV, HD).astype(jnp.float32)
    key_heads = keys_both.reshape(2 * row_count, KV, HD).astype(jnp.float32)
    scores = jnp.einsum('tkgd,skd->kgts', query_heads, key_heads) * (1.0 / math.sqrt(HD))
    scores = jnp.where(visible[None, None], scores, -jnp.inf)
    shifted = scores - lax.optimization_barrier(jnp.max(scores, axis=3, keepdims=True))
    exponent = jnp.exp(shifted)
    weights = (exponent / lax.optimization_barrier(jnp.sum(exponent, axis=3, keepdims=True))).astype(jnp.bfloat16)
    grad_heads = grads_block.reshape(row_count, KV, HEADS // KV, HD).astype(jnp.float32)
    value_terms = jnp.einsum('kgts,tkgd->skd', weights.astype(jnp.float32), grad_heads)
    return value_terms.reshape(2 * row_count, KV * HD)

def block_terms(block_index, queries, key_states, out_grads, lengths):
    sequence = block_index // N_FSDP
    within = block_index % N_FSDP
    doc_ends = jnp.cumsum(lax.dynamic_index_in_dim(lengths, sequence, 0, keepdims=False)).astype(jnp.int32)
    own_pos = (within * TOK_DEV + jnp.arange(TOK_DEV, dtype=jnp.int32)).astype(jnp.int32)
    key_pos = jnp.concatenate([own_pos - TOK_DEV, own_pos]).astype(jnp.int32)
    visible = doc_index(own_pos, doc_ends)[:, None] == doc_index(key_pos, doc_ends)[None, :]
    visible = visible & (key_pos[None, :] <= own_pos[:, None]) & (key_pos[None, :] >= 0)
    start_row = (block_index * TOK_DEV).astype(jnp.int32)
    earlier_row = (jnp.maximum(block_index - 1, 0) * TOK_DEV).astype(jnp.int32)
    keys_both = jnp.concatenate([lax.dynamic_slice_in_dim(key_states, earlier_row, TOK_DEV, 0), lax.dynamic_slice_in_dim(key_states, start_row, TOK_DEV, 0)], axis=0)
    queries_block = lax.dynamic_slice_in_dim(queries, start_row, TOK_DEV, 0)
    grads_block = lax.dynamic_slice_in_dim(out_grads, start_row, TOK_DEV, 0)
    return attend(queries_block, keys_both, grads_block, visible)

def reference(activations, queries, key_states, out_grads, projector, lengths):
    blocks = jnp.arange(N_DP * N_FSDP, dtype=jnp.int32)
    terms = lax.map(lambda block_index: block_terms(block_index, queries, key_states, out_grads, lengths), blocks)
    earlier = terms[:, :TOK_DEV]
    later_part = terms[:, TOK_DEV:]
    from_next = jnp.concatenate([earlier[1:], jnp.zeros_like(earlier[:1])], axis=0)
    has_next = (blocks + 1) % N_FSDP != 0
    from_next = jnp.where(has_next[:, None, None], from_next, jnp.zeros_like(from_next))
    value_grads = (later_part + from_next).reshape(TOKENS, KV * HD).astype(jnp.bfloat16)
    projected = jnp.dot(activations.astype(jnp.float32), projector.astype(jnp.float32), precision=lax.Precision.HIGHEST)
    gradient = jnp.dot(projected.T, value_grads.astype(jnp.float32), precision=lax.Precision.HIGHEST)
    gradient = gradient * (1.0 / math.sqrt(TOKENS))
    return (value_grads, gradient)
```

```python
import functools
import math

import jax
import jax.numpy as jnp
from jax import lax
from jax.experimental import pallas as pl
from jax.experimental.pallas import tpu as pltpu
from jax.sharding import PartitionSpec as P

HEADS = 32
KV = 4
HD = 128
GROUP = HEADS // KV
MESH = pl.DeviceIdType.MESH

NX, NY, NH, NL = 4, 8, 2, 6
NZ = NH * NL
BF = jnp.bfloat16
F32 = jnp.float32


def slot_of(k, o):
    return k * 2 + o


def kernel(
    scale,
    act_hbm, q_hbm, k_hbm, og_hbm, p_hbm, len_ref,
    vg_ref, grad_ref,
    q_v, og_v, kboth, a_all, p_all, terms, prev_send, prev_recv, v_all, acc,
    lhs, core_send, core_recv, x_keep, x_send, x_recv, y_keep, y_send, y_recv,
    z_send, z_recv, g_all,
    lsem, asem_s, asem_r, ksem, xsem_s, xsem_r, ysem_s, ysem_r, zsem_s, zfsem_s, zsem_r,
    psem, vsem, csem, rxs, rxr, rys, ryr, rzs, rzr, rgs, rgr,
):
    dp = lax.axis_index("dp")
    me = lax.axis_index("fsdp")
    x, half, core = dp // 4, (dp // 2) % 2, dp % 2
    y, lo = me % NY, me // NY
    z = half * NL + lo
    par = y % 2
    qa, qb = 2 * par, 2 * par + 1
    ma, mb = 2 - 2 * par, 3 - 2 * par

    def dev(xx, yy, zz, cc):
        return ((xx * 2 + zz // NL) * 2 + cc, (zz % NL) * NY + yy)

    def x_dev(k):
        return dev((x + k) % NX, y, z, core)

    def y_dev(k):
        return dev(x, (y + k) % NY, z, core)

    def z_dev(k):
        return dev(x, y, (z + k) % NZ, core)

    mate = dev(x, y, z, 1 - core)
    has_prev, has_next = me > 0, me < NY * NL - 1

    def remote(src, dst, ssem, rsem, to):
        return pltpu.make_async_remote_copy(
            src_ref=src, dst_ref=dst, send_sem=ssem, recv_sem=rsem, device_id=to, device_id_type=MESH
        )

    def a_cols(k, o, cc):
        blk = (((x + k) % NX) * 2 + (half + o) % 2) * 2 + cc
        return pl.ds(pl.multiple_of(blk * 512, 512), 512)

    def own_rows():
        return pl.ds(0, 128)

    loads = [
        pltpu.make_async_copy(k_hbm, kboth.at[pl.ds(128, 128)], lsem.at[0]),
        pltpu.make_async_copy(q_hbm, q_v, lsem.at[1]),
        pltpu.make_async_copy(og_hbm, og_v, lsem.at[2]),
        pltpu.make_async_copy(p_hbm, p_all.at[0], lsem.at[3]),
    ]
    a_loads = [
        pltpu.make_async_copy(
            act_hbm.at[:, a_cols(s // 2, s % 2, core)], a_all.at[s, pl.ds(0, 128)], lsem.at[4 + s]
        )
        for s in range(8)
    ]
    for c in loads:
        c.start()

    barrier = pltpu.get_barrier_semaphore()
    peers = [mate]
    peers += [x_dev(k) for k in range(1, NX)]
    peers += [y_dev(k) for k in range(1, NY)]
    peers += [z_dev(k) for k in range(1, NZ)]
    for to in peers:
        pl.semaphore_signal(barrier, inc=1, device_id=to, device_id_type=MESH)
    cross_next = jnp.logical_and(y == NY - 1, lo < NL - 1)
    cross_prev = jnp.logical_and(y == 0, lo > 0)

    @pl.when(cross_next)
    def _():
        pl.semaphore_signal(barrier, inc=1, device_id=(dp, me + 1), device_id_type=MESH)

    @pl.when(cross_prev)
    def _():
        pl.semaphore_signal(barrier, inc=1, device_id=(dp, me - 1), device_id_type=MESH)

    for c in a_loads:
        c.start()

    n_docs = len_ref.shape[1]
    lens = jnp.broadcast_to(len_ref[...].astype(F32), (128, n_docs)).astype(BF)
    upto = (
        lax.broadcasted_iota(jnp.int32, (n_docs, n_docs), 1)
        <= lax.broadcasted_iota(jnp.int32, (n_docs, n_docs), 0)
    )
    ends = lax.dot_general(
        jnp.where(upto, 1.0, 0.0).astype(BF), lens, (((1,), (1,)), ((), ())), preferred_element_type=F32
    ).astype(jnp.int32)
    q_pos = me * 128 + lax.broadcasted_iota(jnp.int32, (n_docs, 128), 1)
    start = jnp.max(jnp.where(ends <= q_pos, ends, 0), axis=0, keepdims=True)
    key_pos = (me - 1) * 128 + lax.broadcasted_iota(jnp.int32, (256, 128), 0)
    qry_pos = me * 128 + lax.broadcasted_iota(jnp.int32, (256, 128), 1)
    visible = jnp.logical_and(
        jnp.logical_and(key_pos >= start, key_pos <= qry_pos), key_pos >= 0
    )
    visible2 = jnp.concatenate([visible, visible], axis=1)

    @pl.when(jnp.logical_not(has_prev))
    def _():
        kboth[pl.ds(0, 128), :] = jnp.zeros((128, KV * HD), BF)

    @pl.when(jnp.logical_not(has_next))
    def _():
        prev_recv[...] = jnp.zeros((128, KV * HD), BF)

    pl.semaphore_wait(
        barrier, len(peers) + cross_next.astype(jnp.int32) + cross_prev.astype(jnp.int32)
    )

    k_copy = remote(k_hbm, kboth.at[pl.ds(0, 128)], ksem.at[0], ksem.at[1], (dp, me + 1))

    @pl.when(has_next)
    def _():
        k_copy.start()

    def quarter(q):
        return p_hbm.at[pl.ds(pl.multiple_of(q * 128, 128), 128)]

    def p_part(s, q):
        return p_all.at[s, pl.ds(pl.multiple_of(q * 128, 128), 128)]

    def x_copy(o, m):
        q = qa if m in (0, 3, 4) else qb
        k, dst = ((1, 3), (1, 3), (-1, 1), (-1, 1), (1, 2), (-1, 2))[m]
        if m < 4:
            src = quarter(q) if o == 0 else p_part(slot_of(0, 1), q)
        else:
            src = p_part(slot_of(3 if m == 4 else 1, o), q)
        return remote(
            src, p_part(slot_of(dst, o), q), xsem_s.at[o, m], xsem_r.at[o, m], x_dev(k)
        )

    def y_copy(s, m):
        q = qb if m else qa
        return remote(
            p_part(s, q), p_part(s, q), ysem_s.at[s, m], ysem_r.at[s, m], y_dev(-1 if m else 1)
        )

    def y_wait(s):
        for m, q in ((0, ma), (1, mb)):
            remote(
                p_part(s, q), p_part(s, q), ysem_s.at[s, m], ysem_r.at[s, m], y_dev(-1 if m else 1)
            ).wait_recv()

    low_side = lo < 3
    z_away = jnp.where(low_side, 1, NZ - 1)
    z_out = jnp.where(lo == 0, NZ - 1, 1)
    z_edge = jnp.logical_or(lo == 0, lo == NL - 1)
    z_mid = jnp.logical_or(lo == 2, lo == 3)
    z_second = jnp.logical_or(lo == 1, lo == 4)

    def z_own(m):
        q = qb if m else qa
        return remote(
            quarter(q), p_part(1, q), zsem_s.at[m], zsem_r.at[m], dev(x, y, (z + z_out) % NZ, core)
        )

    def z_on(m):
        q = qb if m else qa
        return remote(
            p_part(1, q), p_part(1, q), zfsem_s.at[m], zsem_r.at[m], dev(x, y, (z + z_away) % NZ, core)
        )

    @pl.when(z_edge)
    def _():
        z_own(0).start()
        z_own(1).start()

    for m in (0, 2, 1, 3):
        x_copy(0, m).start()

    a_copies = [
        remote(
            act_hbm.at[:, a_cols(s // 2, s % 2, 1 - core)],
            a_all.at[s, pl.ds(128, 128)],
            asem_s.at[s],
            asem_r.at[s],
            mate,
        )
        for s in range(8)
    ]
    for c in a_copies:
        c.start()

    def z_step(m):
        z_copy = z_on(m)
        z_copy.wait_recv()

        @pl.when(jnp.logical_not(z_mid))
        def _():
            z_copy.start()

        for mm in ((0, 3), (1, 2))[m]:
            x_copy(1, mm).start()
        y_copy(1, m).start()

    def x_first(o):
        x_copy(o, 0).wait_recv()
        x_copy(o, 4).start()
        y_copy(slot_of(3, o), 0).start()
        x_copy(o, 2).wait_recv()
        x_copy(o, 5).start()
        y_copy(slot_of(1, o), 1).start()

    def x_second(o):
        x_copy(o, 1).wait_recv()
        y_copy(slot_of(3, o), 1).start()
        x_copy(o, 3).wait_recv()
        y_copy(slot_of(1, o), 0).start()

    def x_third(o):
        x_copy(o, 4).wait_recv()
        y_copy(slot_of(2, o), 0).start()
        x_copy(o, 5).wait_recv()
        y_copy(slot_of(2, o), 1).start()

    factor = math.log2(math.e) / math.sqrt(HD)

    def attend(g):
        keys = kboth[:, g * HD : (g + 1) * HD]
        total = jnp.zeros((256, HD), F32)
        for pair in range(GROUP // 2):
            h0 = (g * GROUP + 2 * pair) * HD
            qs = jnp.concatenate([q_v[:, h0 : h0 + HD], q_v[:, h0 + HD : h0 + 2 * HD]], axis=0)
            gs = jnp.concatenate([og_v[:, h0 : h0 + HD], og_v[:, h0 + HD : h0 + 2 * HD]], axis=0)
            s = lax.dot_general(keys, qs, (((1,), (1,)), ((), ())), preferred_element_type=F32)
            s = jnp.where(visible2, s, -jnp.inf)
            e = jnp.exp2((s - jnp.max(s, axis=0, keepdims=True)) * factor)
            w = (e * (1.0 / jnp.sum(e, axis=0, keepdims=True))).astype(BF)
            total = total + jnp.dot(w, gs, preferred_element_type=F32)
        terms[:, g * HD : (g + 1) * HD] = total[128:]
        prev_send[:, g * HD : (g + 1) * HD] = total[:128].astype(BF)

    for c in loads[:3]:
        c.wait()
    x_first(0)

    @pl.when(has_prev)
    def _():
        k_copy.wait_recv()

    attend(0)
    attend(1)

    @pl.when(z_edge)
    def _():
        z_step(0)

    x_second(0)
    attend(2)

    @pl.when(z_edge)
    def _():
        z_step(1)

    attend(3)
    prev_copy = remote(prev_send, prev_recv, psem.at[0], psem.at[1], (dp, me - 1))

    @pl.when(has_prev)
    def _():
        prev_copy.start()

    x_third(0)

    @pl.when(z_second)
    def _():
        z_step(0)
        z_step(1)

    loads[3].wait()
    for c in a_loads:
        c.wait()
    for c in a_copies:
        c.wait_recv()

    def project(s):
        return jnp.dot(a_all[s], p_all[s], preferred_element_type=F32)

    acc[...] = project(0)

    @pl.when(has_next)
    def _():
        prev_copy.wait_recv()

    grads = (terms[...] + prev_recv[...].astype(F32)).astype(BF)
    vg_ref[...] = grads
    v_all[pl.ds(0, 128), :] = grads
    v_copy = remote(
        v_all.at[pl.ds(0, 128)], v_all.at[pl.ds(128, 128)], vsem.at[0], vsem.at[1], mate
    )
    v_copy.start()

    @pl.when(z_mid)
    def _():
        z_step(0)
        z_step(1)

    x_first(1)
    y_wait(slot_of(3, 0))
    acc[...] += project(slot_of(3, 0))
    y_wait(slot_of(1, 0))
    acc[...] += project(slot_of(1, 0))
    x_second(1)
    y_wait(slot_of(2, 0))
    acc[...] += project(slot_of(2, 0))
    x_third(1)
    for k in (0, 3, 1, 2):
        y_wait(slot_of(k, 1))
        acc[...] += project(slot_of(k, 1))

    flipped = acc[...].T
    high = flipped.astype(BF)
    low = (flipped - high.astype(F32)).astype(BF)
    for b in range(16):
        rows = slice(b // 2 * 32, b // 2 * 32 + 32)
        lhs[b % 2, rows, :256] = high[b * 32 : b * 32 + 32]
        lhs[b % 2, rows, 256:] = low[b * 32 : b * 32 + 32]
    v_copy.wait_recv()
    values = jnp.concatenate([v_all[...], v_all[...]], axis=0)
    core_send[...] = (jnp.dot(lhs[1 - core], values, preferred_element_type=F32) * scale).astype(BF)
    core_copy = remote(core_send, core_recv, csem.at[0], csem.at[1], mate)
    core_copy.start()
    mine = jnp.dot(lhs[core], values, preferred_element_type=F32) * scale
    core_copy.wait_recv()
    mine = (mine + core_recv[...].astype(F32)).reshape(NX, 64, 512)
    x_keep[...] = mine
    x_send[...] = mine.astype(BF)
    rx = [
        remote(x_send.at[(x + k) % NX], x_recv.at[k - 1], rxs.at[k - 1], rxr.at[k - 1], x_dev(k))
        for k in range(1, NX)
    ]
    for k in (2, 1, 3):
        rx[k - 1].start()
    mine = x_keep[x]
    for k in (1, 3, 2):
        rx[k - 1].wait_recv()
        mine = mine + x_recv[k - 1].astype(F32)
    for yy in range(NY):
        for h in range(NH):
            r0 = h * 32 + yy // 4 * 16
            c0 = yy % 4 * 128
            piece = mine[r0 : r0 + 16, c0 : c0 + 128]
            y_keep[yy, h] = piece
            y_send[yy, h] = piece.astype(BF)
    ry = [
        remote(y_send.at[(y + k) % NY], y_recv.at[k - 1], rys.at[k - 1], ryr.at[k - 1], y_dev(k))
        for k in range(1, NY)
    ]
    for k in (4, 3, 5, 2, 6, 1, 7):
        ry[k - 1].start()
    mine = y_keep[y]
    for k in (1, 7, 2, 6, 3, 5, 4):
        ry[k - 1].wait_recv()
        mine = mine + y_recv[k - 1].astype(F32)
    z_send[...] = mine
    rz = [
        remote(
            z_send.at[((z + k) % NZ) // NL], z_recv.at[k - 1], rzs.at[k - 1], rzr.at[k - 1], z_dev(k)
        )
        for k in range(1, NZ)
    ]
    for k in (6, 5, 7, 4, 8, 3, 9, 2, 10, 1, 11):
        rz[k - 1].start()
    mine = z_send[half]
    for k in (1, 11, 2, 10, 3, 9, 4, 8, 5, 7, 6):
        rz[k - 1].wait_recv()
        mine = mine + z_recv[k - 1]
    g_all[y] = mine
    rg = [
        remote(g_all.at[y], g_all.at[y], rgs.at[k - 1], rgr.at[k - 1], y_dev(k)) for k in range(1, NY)
    ]
    for k in (4, 3, 5, 2, 6, 1, 7):
        rg[k - 1].start()
    for k in range(1, NY):
        sender = (y + NY - k) % NY
        remote(
            g_all.at[sender], g_all.at[sender], rgs.at[k - 1], rgr.at[k - 1], y_dev(k)
        ).wait_recv()
    for yy in range(NY):
        grad_ref[pl.ds(yy // 4 * 16, 16), pl.ds(yy % 4 * 128, 128)] = g_all[yy]

    @pl.when(has_next)
    def _():
        k_copy.wait_send()

    @pl.when(has_prev)
    def _():
        prev_copy.wait_send()

    @pl.when(z_edge)
    def _():
        z_own(0).wait_send()
        z_own(1).wait_send()

    @pl.when(jnp.logical_not(z_mid))
    def _():
        z_on(0).wait_send()
        z_on(1).wait_send()

    for o in range(2):
        for m in range(6):
            x_copy(o, m).wait_send()
    for s in range(1, 8):
        for m in range(2):
            y_copy(s, m).wait_send()
    for c in a_copies + [v_copy, core_copy] + rx + ry + rz + rg:
        c.wait_send()


def local(activations, queries, key_states, out_grads, projector, lengths):
    toks = queries.shape[0]
    scale = 1.0 / math.sqrt(toks * lax.axis_size("dp") * lax.axis_size("fsdp"))
    dma, vmem = pltpu.SemaphoreType.DMA, pltpu.VMEM
    any_spec = pl.BlockSpec(memory_space=pl.ANY)
    vmem_spec = pl.BlockSpec(memory_space=pltpu.VMEM)
    return pl.pallas_call(
        functools.partial(kernel, scale),
        out_shape=(
            jax.ShapeDtypeStruct((toks, KV * HD), BF),
            jax.ShapeDtypeStruct((32, KV * HD), F32),
        ),
        in_specs=[any_spec] * 5 + [vmem_spec],
        out_specs=(vmem_spec, vmem_spec),
        scratch_shapes=[
            vmem((toks, HEADS * HD), BF),
            vmem((toks, HEADS * HD), BF),
            vmem((2 * toks, KV * HD), BF),
            vmem((8, 2 * toks, 512), BF),
            vmem((8, 512, 512), BF),
            vmem((toks, KV * HD), F32),
            vmem((toks, KV * HD), BF),
            vmem((toks, KV * HD), BF),
            vmem((2 * toks, KV * HD), BF),
            vmem((2 * toks, 512), F32),
            vmem((2, 256, 512), BF),
            vmem((256, 512), BF),
            vmem((256, 512), BF),
            vmem((NX, 64, 512), F32),
            vmem((NX, 64, 512), BF),
            vmem((NX - 1, 64, 512), BF),
            vmem((NY, NH, 16, 128), F32),
            vmem((NY, NH, 16, 128), BF),
            vmem((NY - 1, NH, 16, 128), BF),
            vmem((NH, 16, 128), F32),
            vmem((NZ - 1, 16, 128), F32),
            vmem((NY, 16, 128), F32),
            dma((12,)),
            dma((8,)),
            dma((8,)),
            dma((2,)),
            dma((2, 6)),
            dma((2, 6)),
            dma((8, 2)),
            dma((8, 2)),
            dma((2,)),
            dma((2,)),
            dma((2,)),
            dma((2,)),
            dma((2,)),
            dma((2,)),
            dma((NX - 1,)),
            dma((NX - 1,)),
            dma((NY - 1,)),
            dma((NY - 1,)),
            dma((NZ - 1,)),
            dma((NZ - 1,)),
            dma((NY - 1,)),
            dma((NY - 1,)),
        ],
        compiler_params=pltpu.CompilerParams(collective_id=0, has_side_effects=True),
    )(activations, queries, key_states, out_grads, projector, lengths)


def solution(mesh):
    in_specs = (
        P(("dp", "fsdp"), None),
        P(("dp", "fsdp"), None),
        P(("dp", "fsdp"), None),
        P(("dp", "fsdp"), None),
        P("dp", None),
        P("dp", None),
    )
    out_specs = (P(("dp", "fsdp"), None), P("dp", None))
    return jax.shard_map(local, mesh=mesh, in_specs=in_specs, out_specs=out_specs, check_vma=False)
```

```python
import functools
import math

import jax
import jax.numpy as jnp
from jax import lax
from jax.experimental import pallas as pl
from jax.experimental.pallas import tpu as pltpu
from jax.sharding import PartitionSpec as P

HEADS = 32
KV = 4
HD = 128
GROUP = HEADS // KV
MESH = pl.DeviceIdType.MESH

NX, NY, NH, NL = 4, 8, 2, 6
NZ = NH * NL
BF = jnp.bfloat16
F32 = jnp.float32
VMEM_BYTES = 54528 * 1024


def slot_of(k, o):
    return k * 2 + o


def kernel(
    scale,
    act_hbm, q_hbm, k_hbm, og_hbm, p_hbm, len_ref,
    vg_ref, grad_ref,
    q_v, og_v, kboth, a_all, p_all, terms, prev_send, prev_recv, v_all, acc,
    lhs, core_send, core_recv, x_keep, x_send, x_recv, y_keep, y_send, y_recv,
    z_send, z_recv, g_all,
    lsem, asem_s, asem_r, ksem, xsem_s, xsem_r, ysem_s, ysem_r, zsem_s, zfsem_s, zsem_r,
    ytok, ztok, psem, vsem, csem, rxs, rxr, rys, ryr, rzs, rzr, rgs, rgr,
):
    dp = lax.axis_index("dp")
    me = lax.axis_index("fsdp")
    x, half, core = dp // 4, (dp // 2) % 2, dp % 2
    y, lo = me % NY, me // NY
    z = half * NL + lo
    par = y % 2
    qa, qb = 2 * par, 2 * par + 1
    ma, mb = 2 - 2 * par, 3 - 2 * par

    def dev(xx, yy, zz, cc):
        return ((xx * 2 + zz // NL) * 2 + cc, (zz % NL) * NY + yy)

    def x_dev(k):
        return dev((x + k) % NX, y, z, core)

    def y_dev(k):
        return dev(x, (y + k) % NY, z, core)

    def z_dev(k):
        return dev(x, y, (z + k) % NZ, core)

    mate = dev(x, y, z, 1 - core)
    has_prev, has_next = me > 0, me < NY * NL - 1

    def remote(src, dst, ssem, rsem, to):
        return pltpu.make_async_remote_copy(
            src_ref=src, dst_ref=dst, send_sem=ssem, recv_sem=rsem, device_id=to, device_id_type=MESH
        )

    def a_cols(k, o, cc):
        blk = (((x + k) % NX) * 2 + (half + o) % 2) * 2 + cc
        return pl.ds(pl.multiple_of(blk * 512, 512), 512)

    loads = [
        pltpu.make_async_copy(k_hbm, kboth.at[pl.ds(128, 128)], lsem.at[0]),
        pltpu.make_async_copy(q_hbm, q_v, lsem.at[1]),
        pltpu.make_async_copy(og_hbm, og_v, lsem.at[2]),
        pltpu.make_async_copy(p_hbm, p_all.at[0], lsem.at[3]),
    ]
    a_loads = [
        pltpu.make_async_copy(
            act_hbm.at[:, a_cols(s // 2, s % 2, core)], a_all.at[s, pl.ds(0, 128)], lsem.at[4 + s]
        )
        for s in range(8)
    ]
    for c in loads:
        c.start()

    barrier = pltpu.get_barrier_semaphore()
    peers = [mate, x_dev(1), x_dev(-1), x_dev(2), y_dev(1), y_dev(-1), z_dev(1), z_dev(-1)]
    for to in peers:
        pl.semaphore_signal(barrier, inc=1, device_id=to, device_id_type=MESH)
    cross_next = jnp.logical_and(y == NY - 1, lo < NL - 1)
    cross_prev = jnp.logical_and(y == 0, lo > 0)

    @pl.when(cross_next)
    def _():
        pl.semaphore_signal(barrier, inc=1, device_id=(dp, me + 1), device_id_type=MESH)

    @pl.when(cross_prev)
    def _():
        pl.semaphore_signal(barrier, inc=1, device_id=(dp, me - 1), device_id_type=MESH)

    for c in a_loads:
        c.start()

    n_docs = len_ref.shape[1]
    lens = jnp.broadcast_to(len_ref[...].astype(F32), (128, n_docs)).astype(BF)
    upto = (
        lax.broadcasted_iota(jnp.int32, (n_docs, n_docs), 1)
        <= lax.broadcasted_iota(jnp.int32, (n_docs, n_docs), 0)
    )
    ends = lax.dot_general(
        jnp.where(upto, 1.0, 0.0).astype(BF), lens, (((1,), (1,)), ((), ())), preferred_element_type=F32
    ).astype(jnp.int32)
    q_pos = me * 128 + lax.broadcasted_iota(jnp.int32, (n_docs, 128), 1)
    start = jnp.max(jnp.where(ends <= q_pos, ends, 0), axis=0, keepdims=True)
    key_pos = (me - 1) * 128 + lax.broadcasted_iota(jnp.int32, (256, 128), 0)
    qry_pos = me * 128 + lax.broadcasted_iota(jnp.int32, (256, 128), 1)
    visible = jnp.logical_and(
        jnp.logical_and(key_pos >= start, key_pos <= qry_pos), key_pos >= 0
    )
    visible2 = jnp.concatenate([visible, visible], axis=1)

    @pl.when(jnp.logical_not(has_prev))
    def _():
        kboth[pl.ds(0, 128), :] = jnp.zeros((128, KV * HD), BF)

    @pl.when(jnp.logical_not(has_next))
    def _():
        prev_recv[...] = jnp.zeros((128, KV * HD), BF)

    pl.semaphore_wait(
        barrier, len(peers) + cross_next.astype(jnp.int32) + cross_prev.astype(jnp.int32)
    )

    def tokens(axis, r):
        sems, to = ((ytok, y_dev), (ztok, z_dev))[axis]
        return [(sems.at[r, 0], to(1)), (sems.at[r, 1], to(-1))]

    rounds = (NY // 2 - 1, NZ // 2 - 1)

    def token_send(r):
        for axis in range(2):
            if r < rounds[axis]:
                for sem, to in tokens(axis, r):
                    pl.semaphore_signal(sem, inc=1, device_id=to, device_id_type=MESH)

    def token_step(r):
        for axis in range(2):
            if r < rounds[axis]:
                for sem, _ in tokens(axis, r):
                    pl.semaphore_wait(sem, 1)
        token_send(r + 1)

    token_send(0)

    k_copy = remote(k_hbm, kboth.at[pl.ds(0, 128)], ksem.at[0], ksem.at[1], (dp, me + 1))

    @pl.when(has_next)
    def _():
        k_copy.start()

    def rows_of(e):
        side = par if e < 4 else 1 - par
        return pl.ds(pl.multiple_of(side * 256 + e % 4 * 64, 64), 64)

    def p_part(s, e):
        return p_all.at[s, rows_of(e)]

    def x_copy(o, d, e):
        src = p_hbm.at[rows_of(e)] if o == 0 else p_part(slot_of(0, 1), e)
        return remote(
            src,
            p_part(slot_of((3, 1, 2)[d], o), e),
            xsem_s.at[o, d, e],
            xsem_r.at[o, d, e],
            x_dev((1, -1, 2)[d]),
        )

    def y_copy(s, e):
        return remote(
            p_part(s, e), p_part(s, e), ysem_s.at[s, e], ysem_r.at[s, e], y_dev(-1 if e % 2 else 1)
        )

    def y_wait(s):
        for e in range(4):
            remote(
                p_part(s, e + 4), p_part(s, e + 4), ysem_s.at[s, e], ysem_r.at[s, e],
                y_dev(-1 if e % 2 else 1),
            ).wait_recv()

    low_side = lo < 3
    z_away = jnp.where(low_side, 1, NZ - 1)
    z_out = jnp.where(lo == 0, NZ - 1, 1)
    z_edge = jnp.logical_or(lo == 0, lo == NL - 1)
    z_mid = jnp.logical_or(lo == 2, lo == 3)
    z_second = jnp.logical_or(lo == 1, lo == 4)

    def z_own(e):
        return remote(
            p_hbm.at[rows_of(e)], p_part(1, e), zsem_s.at[e], zsem_r.at[e],
            dev(x, y, (z + z_out) % NZ, core),
        )

    def z_on(e):
        return remote(
            p_part(1, e), p_part(1, e), zfsem_s.at[e], zsem_r.at[e],
            dev(x, y, (z + z_away) % NZ, core),
        )

    @pl.when(z_edge)
    def _():
        for e in range(4):
            z_own(e).start()

    for e in range(4):
        for d in range(3):
            x_copy(0, d, e).start()

    @pl.when(z_edge)
    def _():
        for e in range(4, 8):
            z_own(e).start()

    a_copies = [
        remote(
            act_hbm.at[:, a_cols(s // 2, s % 2, 1 - core)],
            a_all.at[s, pl.ds(128, 128)],
            asem_s.at[s],
            asem_r.at[s],
            mate,
        )
        for s in range(8)
    ]
    for c in a_copies:
        c.start()

    def z_step(kind, chunks):
        @pl.when(kind)
        def _():
            for e in chunks:
                z_copy = z_on(e)
                z_copy.wait_recv()
                if kind is not z_mid:
                    z_copy.start()
                if e < 4:
                    for d in (2, 0, 1):
                        x_copy(1, d, e).start()

    def x_step(o, e):
        for d in (0, 1, 2):
            x_copy(o, d, e).wait_recv()
            y_copy(slot_of((3, 1, 2)[d], o), e).start()

    factor = math.log2(math.e) / math.sqrt(HD)

    def attend(g):
        keys = kboth[:, g * HD : (g + 1) * HD]
        total = jnp.zeros((256, HD), F32)
        for pair in range(GROUP // 2):
            h0 = (g * GROUP + 2 * pair) * HD
            qs = jnp.concatenate([q_v[:, h0 : h0 + HD], q_v[:, h0 + HD : h0 + 2 * HD]], axis=0)
            gs = jnp.concatenate([og_v[:, h0 : h0 + HD], og_v[:, h0 + HD : h0 + 2 * HD]], axis=0)
            s = lax.dot_general(keys, qs, (((1,), (1,)), ((), ())), preferred_element_type=F32)
            s = jnp.where(visible2, s, -jnp.inf)
            e = jnp.exp2((s - jnp.max(s, axis=0, keepdims=True)) * factor)
            w = (e * (1.0 / jnp.sum(e, axis=0, keepdims=True))).astype(BF)
            total = total + jnp.dot(w, gs, preferred_element_type=F32)
        terms[:, g * HD : (g + 1) * HD] = total[128:]
        prev_send[:, g * HD : (g + 1) * HD] = total[:128].astype(BF)

    for c in loads[:3]:
        c.wait()
    z_step(z_edge, (0,))
    x_step(0, 0)
    z_step(z_edge, (1,))

    @pl.when(has_prev)
    def _():
        k_copy.wait_recv()

    attend(0)
    z_step(z_edge, (2, 3))
    z_step(z_second, (0,))
    x_step(0, 1)
    attend(1)
    z_step(z_second, (1, 2))
    x_step(0, 2)
    z_step(z_edge, (4, 5))
    attend(2)
    z_step(z_second, (3,))
    z_step(z_mid, (0,))
    x_step(0, 3)
    attend(3)
    prev_copy = remote(prev_send, prev_recv, psem.at[0], psem.at[1], (dp, me - 1))

    @pl.when(has_prev)
    def _():
        prev_copy.start()

    z_step(z_edge, (6, 7))
    z_step(z_mid, (1, 2))
    z_step(z_second, (4, 5))
    z_step(z_mid, (3,))
    z_step(z_second, (6, 7))
    x_step(1, 0)

    loads[3].wait()
    for c in a_loads:
        c.wait()
    for c in a_copies:
        c.wait_recv()

    def project(s):
        return jnp.dot(a_all[s], p_all[s], preferred_element_type=F32)

    acc[...] = project(0)
    token_step(0)
    x_step(1, 1)
    token_step(1)

    @pl.when(has_next)
    def _():
        prev_copy.wait_recv()

    grads = (terms[...] + prev_recv[...].astype(F32)).astype(BF)
    vg_ref[...] = grads
    v_all[pl.ds(0, 128), :] = grads
    v_copy = remote(
        v_all.at[pl.ds(0, 128)], v_all.at[pl.ds(128, 128)], vsem.at[0], vsem.at[1], mate
    )
    v_copy.start()
    x_step(1, 2)
    token_step(2)
    x_step(1, 3)
    token_step(3)
    token_step(4)
    for s in (slot_of(3, 0), slot_of(1, 0), slot_of(2, 0)):
        y_wait(s)
        acc[...] += project(s)
    z_step(z_mid, (4, 5, 6, 7))
    acc[...] += project(slot_of(0, 1))
    for s in (slot_of(3, 1), slot_of(1, 1), slot_of(2, 1)):
        y_wait(s)
        acc[...] += project(s)

    flipped = acc[...].T
    high = flipped.astype(BF)
    low = (flipped - high.astype(F32)).astype(BF)
    for b in range(16):
        at = (b % 2, b // 2 % 2, slice(b // 4 * 32, b // 4 * 32 + 32))
        lhs[at + (slice(0, 256),)] = high[b * 32 : b * 32 + 32]
        lhs[at + (slice(256, 512),)] = low[b * 32 : b * 32 + 32]
    v_copy.wait_recv()
    values = jnp.concatenate([v_all[...], v_all[...]], axis=0)

    halves = (1 - half, half)

    def term(cc, hh):
        return jnp.dot(lhs[cc, hh], values, preferred_element_type=F32) * scale

    rc = [
        remote(core_send.at[t], core_recv.at[t], csem.at[0, t], csem.at[1, t], mate)
        for t in range(2)
    ]
    for t in range(2):
        core_send[t] = term(1 - core, halves[t]).astype(BF)
        rc[t].start()
    rx = [
        [
            remote(
                x_send.at[t, (x + k) % NX], x_recv.at[t, k - 1], rxs.at[t, k - 1], rxr.at[t, k - 1],
                x_dev(k),
            )
            for k in range(1, NX)
        ]
        for t in range(2)
    ]
    ry = [
        [
            remote(
                y_send.at[t, (y + k) % NY], y_recv.at[t, k - 1], rys.at[t, k - 1], ryr.at[t, k - 1],
                y_dev(k),
            )
            for k in range(1, NY)
        ]
        for t in range(2)
    ]
    rz_far = [
        remote(
            z_send.at[0], z_recv.at[k], rzs.at[k], rzr.at[k],
            dev(x, y, (1 - half) * NL + (lo + k) % NL, core),
        )
        for k in range(NL)
    ]
    rz_near = [
        remote(
            z_send.at[1], z_recv.at[NL + k - 1], rzs.at[NL + k - 1], rzr.at[NL + k - 1],
            dev(x, y, half * NL + (lo + k) % NL, core),
        )
        for k in range(1, NL)
    ]
    for t in range(2):
        mine = term(core, halves[t])
        rc[t].wait_recv()
        mine = (mine + core_recv[t].astype(F32)).reshape(NX, 32, 512)
        x_keep[t] = mine
        x_send[t] = mine.astype(BF)
        for k in (2, 1, 3):
            rx[t][k - 1].start()
    for t in range(2):
        mine = x_keep[t, x]
        for k in (1, 3, 2):
            rx[t][k - 1].wait_recv()
            mine = mine + x_recv[t, k - 1].astype(F32)
        for yy in range(NY):
            piece = mine[yy // 4 * 16 : yy // 4 * 16 + 16, yy % 4 * 128 : yy % 4 * 128 + 128]
            y_keep[t, yy] = piece
            y_send[t, yy] = piece.astype(BF)
        for k in (4, 3, 5, 2, 6, 1, 7):
            ry[t][k - 1].start()
    for t in range(2):
        mine = y_keep[t, y]
        for k in (1, 7, 2, 6, 3, 5, 4):
            ry[t][k - 1].wait_recv()
            mine = mine + y_recv[t, k - 1].astype(F32)
        z_send[t] = mine.astype(BF)
        for c in (rz_far, rz_near)[t]:
            c.start()
    for k, c in enumerate(rz_near):
        c.wait_recv()
        mine = mine + z_recv[NL + k].astype(F32)
    for k, c in enumerate(rz_far):
        c.wait_recv()
        mine = mine + z_recv[k].astype(F32)
    g_all[y] = mine
    rg = [
        remote(g_all.at[y], g_all.at[y], rgs.at[k - 1], rgr.at[k - 1], y_dev(k)) for k in range(1, NY)
    ]
    for k in (4, 3, 5, 2, 6, 1, 7):
        rg[k - 1].start()
    for k in range(1, NY):
        sender = (y + NY - k) % NY
        remote(
            g_all.at[sender], g_all.at[sender], rgs.at[k - 1], rgr.at[k - 1], y_dev(k)
        ).wait_recv()
    for yy in range(NY):
        grad_ref[pl.ds(yy // 4 * 16, 16), pl.ds(yy % 4 * 128, 128)] = g_all[yy]

    @pl.when(has_next)
    def _():
        k_copy.wait_send()

    @pl.when(has_prev)
    def _():
        prev_copy.wait_send()

    @pl.when(z_edge)
    def _():
        for e in range(8):
            z_own(e).wait_send()

    @pl.when(jnp.logical_not(z_mid))
    def _():
        for e in range(8):
            z_on(e).wait_send()

    for o in range(2):
        for e in range(4):
            for d in range(3):
                x_copy(o, d, e).wait_send()
    for s in range(2, 8):
        for e in range(4):
            y_copy(s, e).wait_send()
    for c in a_copies + [v_copy] + rc + rx[0] + rx[1] + ry[0] + ry[1] + rz_far + rz_near + rg:
        c.wait_send()


def local(activations, queries, key_states, out_grads, projector, lengths):
    toks = queries.shape[0]
    scale = 1.0 / math.sqrt(toks * lax.axis_size("dp") * lax.axis_size("fsdp"))
    dma, vmem = pltpu.SemaphoreType.DMA, pltpu.VMEM
    any_spec = pl.BlockSpec(memory_space=pltpu.HBM)
    vmem_spec = pl.BlockSpec(memory_space=pltpu.VMEM)
    return pl.pallas_call(
        functools.partial(kernel, scale),
        out_shape=(
            jax.ShapeDtypeStruct((toks, KV * HD), BF),
            jax.ShapeDtypeStruct((32, KV * HD), F32),
        ),
        in_specs=[any_spec] * 5 + [vmem_spec],
        out_specs=(vmem_spec, vmem_spec),
        scratch_shapes=[
            vmem((toks, HEADS * HD), BF),
            vmem((toks, HEADS * HD), BF),
            vmem((2 * toks, KV * HD), BF),
            vmem((8, 2 * toks, 512), BF),
            vmem((8, 512, 512), BF),
            vmem((toks, KV * HD), F32),
            vmem((toks, KV * HD), BF),
            vmem((toks, KV * HD), BF),
            vmem((2 * toks, KV * HD), BF),
            vmem((2 * toks, 512), F32),
            vmem((2, NH, 128, 512), BF),
            vmem((2, 128, 512), BF),
            vmem((2, 128, 512), BF),
            vmem((2, NX, 32, 512), F32),
            vmem((2, NX, 32, 512), BF),
            vmem((2, NX - 1, 32, 512), BF),
            vmem((2, NY, 16, 128), F32),
            vmem((2, NY, 16, 128), BF),
            vmem((2, NY - 1, 16, 128), BF),
            vmem((2, 16, 128), BF),
            vmem((NZ - 1, 16, 128), BF),
            vmem((NY, 16, 128), F32),
            dma((12,)),
            dma((8,)),
            dma((8,)),
            dma((2,)),
            dma((2, 3, 4)),
            dma((2, 3, 4)),
            dma((8, 4)),
            dma((8, 4)),
            dma((8,)),
            dma((8,)),
            dma((8,)),
            pltpu.SemaphoreType.REGULAR((NY // 2 - 1, 2)),
            pltpu.SemaphoreType.REGULAR((NZ // 2 - 1, 2)),
            dma((2,)),
            dma((2,)),
            dma((2, 2)),
            dma((2, NX - 1)),
            dma((2, NX - 1)),
            dma((2, NY - 1)),
            dma((2, NY - 1)),
            dma((NZ - 1,)),
            dma((NZ - 1,)),
            dma((NY - 1,)),
            dma((NY - 1,)),
        ],
        compiler_params=pltpu.CompilerParams(
            collective_id=0, has_side_effects=True, vmem_limit_bytes=VMEM_BYTES
        ),
    )(activations, queries, key_states, out_grads, projector, lengths)


def solution(mesh):
    in_specs = (
        P(("dp", "fsdp"), None),
        P(("dp", "fsdp"), None),
        P(("dp", "fsdp"), None),
        P(("dp", "fsdp"), None),
        P("dp", None),
        P("dp", None),
    )
    out_specs = (P(("dp", "fsdp"), None), P("dp", None))
    return jax.shard_map(local, mesh=mesh, in_specs=in_specs, out_specs=out_specs, check_vma=False)
```
